32 devices in a mesh: fsdp: 4 (over x, core), roll: 8 (over z, y).
Axes of the slice: x: 2, y: 2, z: 4, core: 2. Of those that a mesh axis runs over, the one named last changes fastest.
Arguments:
- trainer_weights: bfloat16 [8, 1024, 8192], P('roll', None, 'fsdp'), may hold values from -0.09375 to 0.09375
- power_table: int32 [8192, 512], P('fsdp'), may hold values from 1 to 250, as said below
- assign: int32 [2], replicated, may hold values from 0 to 7
Outputs:
- rollout_weights: bfloat16 [8, 2, 1024, 8192], P('roll', None, 'fsdp')
- fingerprint: bfloat16 [8, 2, 1024, 512], P('roll', None, 'fsdp')
The draws below stay inside these ranges and needn't reach their ends.
Inputs may be any that keep to these rules, and one draw needn't show every extreme that they name: `power_table`: each entry is, modulo 251, a row factor times a column factor times the column's generator raised to the row index.
All inputs are finite; a program needn't handle non-finite values.
Results may differ from the reference program's by a relative error of at most 0.019.
Values may be sent and summed in bfloat16 or wider, within the bound.
A program may use at most 64 MiB of HBM per device.

```python
import jax
import jax.numpy as jnp
from jax import lax

D = 8192
COLS = 1024
FP = 512
LAYERS = 2
N_FSDP = 4
N_ROLL = 8


def draw_power_table(key, part):
    subkeys = jax.random.split(jax.random.fold_in(key, 7), 3)
    generators = jax.random.randint(subkeys[0], (FP,), 2, 251)
    column_factor = jax.random.randint(subkeys[1], (FP,), 1, 251)
    row_factor = jax.random.randint(subkeys[2], (D,), 1, 251)
    exponent = jnp.arange(D, dtype=jnp.int32)
    result = jnp.ones((D, FP), jnp.int32)
    powered = generators.astype(jnp.int32)
    for position in range(16):
        chosen_bit = exponent // 2 ** position % 2
        factor = jnp.where(chosen_bit[:, None] == 1, powered[None, :], 1)
        result = result * factor % 251
        powered = powered * powered % 251
    result = result * row_factor[:, None] % 251
    return result * column_factor[None, :] % 251


def with_spikes(values, stream_key, source, target, blocks, factor):
    def block_of(axis_at):
        return (jnp.arange(values.shape[axis_at]) // (values.shape[axis_at] // blocks)).reshape((-1,) + (1,) * (values.ndim - 1 - axis_at))

    near = jax.random.permutation(stream_key, blocks)[block_of(target)]
    far = (block_of(target) + blocks // 2) % blocks
    return jnp.where((block_of(source) == near) | (block_of(source) == far), factor * values, values)


def block_scale(rng, shape, cuts, low, largest):
    level, own = 1.0, jax.random.fold_in(rng, 6)
    for dim, parts in cuts:
        steps = jnp.exp(jax.random.uniform(jax.random.fold_in(own, dim), (parts,), jnp.float32, low / len(cuts), largest / len(cuts)))
        level = level * jnp.repeat(steps, shape[dim] // parts).reshape([-1 if axis == dim else 1 for axis in range(len(shape))])
    return level


def noise_with(stream_key, extent, width, limit, cuts, heavy, kind=jnp.bfloat16):
    values = width * jax.random.normal(stream_key, extent, jnp.float32)
    if cuts:
        values = values * block_scale(stream_key, extent, cuts, -0.22, 0.18)
    return jnp.clip(with_spikes(values, jax.random.fold_in(stream_key, 3), *heavy), -limit, limit).astype(kind)


def setup_inputs(seed: int = 0) -> dict:
    seeds = jax.random.split(jax.random.key(seed), 4)
    trainer_weights = noise_with(seeds[0], (N_ROLL, COLS, D), D ** -0.5, 0.09375, ((0, 8), (2, 4)), (2, 1, 4, 2.0))
    power_table = draw_power_table(jax.random.fold_in(seeds[3], 71), 0)
    assign = jax.random.randint(seeds[2], (LAYERS,), 0, N_ROLL).astype(jnp.int32)
    return dict(trainer_weights=trainer_weights, power_table=power_table, assign=assign)


spread_inverse = 1.0 / 72.0


def reference(trainer_weights, power_table, assign):
    centered = (power_table - 125).astype(jnp.float32)
    blocks = centered.reshape(N_FSDP, D // N_FSDP, FP)
    rollout = []
    prints = []
    for number in range(LAYERS):
        chosen = lax.dynamic_index_in_dim(trainer_weights, assign[number], 0, keepdims=False)
        rollout.append(chosen)
        pieces = chosen.astype(jnp.float32).reshape(COLS, N_FSDP, D // N_FSDP)
        partial_value = jnp.einsum("cjd,jdf->jcf", pieces, blocks, precision=lax.Precision.HIGHEST).astype(jnp.bfloat16)
        summed = jnp.sum(partial_value.astype(jnp.float32), axis=0)
        prints.append((summed * spread_inverse).astype(jnp.bfloat16))
    stacked = jnp.stack(rollout)
    printed = jnp.stack(prints)
    copies = jnp.broadcast_to(stacked[None], (N_ROLL,) + stacked.shape)
    print_copies = jnp.broadcast_to(printed[None], (N_ROLL,) + printed.shape)
    return copies, print_copies
```

```python
import functools

import jax
import jax.numpy as jnp
from jax import lax
from jax.experimental import pallas as pl
from jax.experimental.pallas import tpu as pltpu
from jax.sharding import PartitionSpec as P

spread_inverse = 1.0 / 72.0
CHUNKS = 8
MOST_SOURCES = 16
MESH = pl.DeviceIdType.MESH


def flip(index, mask):
    bit = 1
    while bit <= mask:
        if mask & bit:
            index = index + bit - 2 * bit * ((index // bit) % 2)
        bit *= 2
    return index


def powers_below(limit):
    bit, found = 1, []
    while bit < limit:
        found.append(bit)
        bit *= 2
    return found


def broadcast_kernel(n_roll, n_fsdp, source, chunks, with_table, *refs):
    if with_table:
        (w_ref, tab_ref, out_ref, all_ref, stage, local_sem, recv_sem, send_sem, swap_sem, t_local, t_recv, t_send) = refs
    else:
        w_ref, out_ref, stage, local_sem, recv_sem, send_sem, swap_sem = refs
    r, f = lax.axis_index("roll"), lax.axis_index("fsdp")
    half, rungs = n_fsdp // 2, n_roll // 2
    k, b = r // 2, r % 2
    ks, bs = source // 2, source % 2
    pivot = 2 * ks + 1 - bs
    inner = ks + 1 if ks + 1 < rungs else ks - 1
    relay = 2 * inner + 1 - bs
    rows, depth = out_ref.shape[0], w_ref.shape[1]
    height = rows // chunks
    is_source = r == source

    def piece(stream, c, i):
        owner = flip(f, stream * half + i)
        return out_ref.at[
            pl.ds(pl.multiple_of(c * height, height), height),
            pl.ds(pl.multiple_of(owner * depth, 128), depth),
        ]

    def mine(c, owner):
        return w_ref.at[pl.ds(pl.multiple_of(owner * rows + c * height, height), height), :]

    def move(stream, c, i, slot, to, own=False):
        q = c * half + i
        return pltpu.make_async_remote_copy(
            src_ref=mine(c, f) if own else piece(stream, c, i),
            dst_ref=piece(stream, c, i),
            send_sem=send_sem.at[stream, slot, q],
            recv_sem=recv_sem.at[stream, q],
            device_id={"roll": to, "fsdp": f},
            device_id_type=MESH,
        )

    def swap(c, m):
        peer = flip(f, m)
        dst = out_ref.at[
            pl.ds(pl.multiple_of(c * height, height), height),
            pl.ds(pl.multiple_of(f * depth, 128), depth),
        ]
        return pltpu.make_async_remote_copy(
            src_ref=mine(c, peer),
            dst_ref=dst,
            send_sem=swap_sem.at[m - 1, c],
            recv_sem=recv_sem.at[m // half, c * half + m % half],
            device_id={"roll": r, "fsdp": peer},
            device_id_type=MESH,
        )

    def arrived(stream, c, i):
        move(stream, c, i, 0, r).wait_recv()

    def each(body, count=chunks):
        def step(c, carry):
            body(c)
            return carry

        lax.fori_loop(0, count, step, 0)

    up = jnp.logical_and(k >= ks, k + 1 < rungs)
    down = jnp.logical_and(k <= ks, k >= 1)

    t_rows = depth // chunks

    def t_block(c, owner):
        return all_ref.at[pl.ds(pl.multiple_of(owner * depth + c * t_rows, t_rows), t_rows), :]

    def t_move(c, m, slot, to_roll, to_fsdp, m_there):
        owner = flip(f, m)
        src = tab_ref.at[pl.ds(pl.multiple_of(c * t_rows, t_rows), t_rows), :] if m == 0 else t_block(c, owner)
        return pltpu.make_async_remote_copy(
            src_ref=src,
            dst_ref=t_block(c, owner),
            send_sem=t_send.at[m, slot, c],
            recv_sem=t_recv.at[m_there, c],
            device_id={"roll": to_roll, "fsdp": to_fsdp},
            device_id_type=MESH,
        )

    bits = powers_below(n_fsdp)

    def t_own(c, finish):
        for slot, e in enumerate(bits):
            def go(e=e, slot=slot):
                copy = t_move(c, 0, slot, r, flip(f, e), e)
                copy.wait_send() if finish else copy.start()

            if e == half:
                pl.when(jnp.logical_not(is_source))(go)
            else:
                go()

    def t_pass(c, finish):
        for m in range(1, n_fsdp):
            if not finish:
                t_move(c, m, 0, r, f, m).wait_recv()
            for slot, e in enumerate(powers_below(m & -m)):
                copy = t_move(c, m, slot, r, flip(f, e), m + e)
                copy.wait_send() if finish else copy.start()
            if m == half:

                @pl.when(r == pivot)
                def _():
                    copy = t_move(c, m, len(bits), source, f, m)
                    copy.wait_send() if finish else copy.start()

    lag = 2

    def table_step(c):
        if with_table:

            @pl.when(c >= lag)
            def _():
                t_pass(c - lag, False)

    if with_table:
        keep = pltpu.make_async_copy(
            tab_ref, all_ref.at[pl.ds(pl.multiple_of(f * depth, depth), depth), :], t_local
        )
        keep.start()

    @pl.when(is_source)
    def _():
        load = pltpu.make_async_copy(w_ref.at[pl.ds(pl.multiple_of(f * rows, rows), rows), :], stage, local_sem.at[0])
        store = pltpu.make_async_copy(stage, out_ref.at[:, pl.ds(pl.multiple_of(f * depth, 128), depth)], local_sem.at[1])
        load.start()
        ways = ([(0, source + 2)] if ks + 1 < rungs else []) + ([(1, source - 2)] if ks >= 1 else [])

        def begin(c):
            for m in list(range(half, n_fsdp)) + list(range(1, half)):
                swap(c, m).start()
            for slot, to in ways:
                move(0, c, 0, slot, to, own=True).start()
            if with_table:
                t_own(c, False)

        each(begin)

        def step(c):
            for i in range(1, half):
                arrived(0, c, i)
                for slot, to in ways:
                    move(0, c, i, slot, to).start()
            for i in range(half):
                arrived(1, c, i)
                move(1, c, i, 2, pivot).start()
            table_step(c)

        each(step)
        load.wait()
        store.start()
        store.wait()

        def finish(c):
            for m in range(1, n_fsdp):
                swap(c, m).wait_send()
            for slot, to in ways:
                for i in range(half):
                    move(0, c, i, slot, to, own=i == 0).wait_send()
            for i in range(half):
                move(1, c, i, 2, pivot).wait_send()

        each(finish)

    def carry_on(stream, c, i, finish):
        def do(slot, to):
            copy = move(stream, c, i, slot, to)
            copy.wait_send() if finish else copy.start()

        pl.when(up)(lambda: do(0, r + 2))
        pl.when(down)(lambda: do(1, r - 2))
        pl.when(k != ks)(lambda: do(2, r + 1 - 2 * b))

    @pl.when(jnp.logical_not(is_source))
    def _():
        if with_table:
            each(lambda c: t_own(c, False))

    @pl.when(jnp.logical_and(b == bs, k != ks))
    def _():
        def step(c):
            for i in range(half):
                arrived(0, c, i)
                carry_on(0, c, i, False)
            table_step(c)

        each(step)

        def finish(c):
            for i in range(half):
                arrived(1, c, i)
                carry_on(0, c, i, True)

        each(finish)

    @pl.when(b != bs)
    def _():
        def step(c):
            for i in range(half):

                @pl.when(r == relay)
                def _():
                    arrived(0, c, i)
                    move(0, c, i, 0, pivot).start()

                arrived(1, c, i)
                carry_on(1, c, i, False)
            table_step(c)

        each(step)

        def finish(c):
            for i in range(half):

                @pl.when(r == relay)
                def _():
                    move(0, c, i, 0, pivot).wait_send()

                @pl.when(r != relay)
                def _():
                    arrived(0, c, i)

                carry_on(1, c, i, True)

        each(finish)

    if with_table:
        each(lambda c: t_pass(c + chunks - lag, False), lag)

        def finish(c):
            t_own(c, True)
            t_pass(c, True)

        each(finish)
        keep.wait()


def broadcast(n_roll, n_fsdp, source, layer, own_block, table):
    rows, depth = own_block.shape[0] // n_fsdp, own_block.shape[1]
    half = n_fsdp // 2
    chunks = min(CHUNKS, rows // 16)
    with_table = table is not None
    anywhere = pl.BlockSpec(memory_space=pl.ANY)
    out_shape = [jax.ShapeDtypeStruct((rows, depth * n_fsdp), own_block.dtype)]
    in_specs = [anywhere]
    scratch = [
        pltpu.VMEM((rows, depth), own_block.dtype),
        pltpu.SemaphoreType.DMA((2,)),
        pltpu.SemaphoreType.DMA((2, chunks * half)),
        pltpu.SemaphoreType.DMA((2, 3, chunks * half)),
        pltpu.SemaphoreType.DMA((n_fsdp - 1, chunks)),
    ]
    operands = [own_block]
    if with_table:
        out_shape.append(jax.ShapeDtypeStruct((depth * n_fsdp, table.shape[1]), table.dtype))
        in_specs.append(pl.BlockSpec(memory_space=pltpu.VMEM))
        scratch += [
            pltpu.SemaphoreType.DMA,
            pltpu.SemaphoreType.DMA((n_fsdp, chunks)),
            pltpu.SemaphoreType.DMA((n_fsdp, len(powers_below(n_fsdp)) + 1, chunks)),
        ]
        operands.append(table)
    return pl.pallas_call(
        functools.partial(broadcast_kernel, n_roll, n_fsdp, source, chunks, with_table),
        out_shape=out_shape,
        in_specs=in_specs,
        out_specs=[anywhere] * len(out_shape),
        scratch_shapes=scratch,
        name=f"broadcast_{layer}_{source}",
        compiler_params=pltpu.CompilerParams(has_side_effects=True),
    )(*operands)


def spread(block, axis, source):
    block = jnp.where(lax.axis_index(axis) == source, block, jnp.zeros_like(block))
    return lax.psum(block, axis)


def by_sums(own_block, centered, assign):
    regrouped = lax.all_to_all(own_block, "fsdp", split_axis=0, concat_axis=1, tiled=True)
    summed = lax.psum_scatter(
        jnp.dot(own_block, centered, preferred_element_type=jnp.float32).astype(jnp.bfloat16),
        "fsdp",
        scatter_dimension=0,
        tiled=True,
    ).astype(jnp.float32)
    printed = (summed * spread_inverse).astype(jnp.bfloat16)
    layers = range(assign.shape[0])
    return (
        jnp.stack([spread(regrouped, "roll", assign[number]) for number in layers])[None],
        jnp.stack([spread(printed, "roll", assign[number]) for number in layers])[None],
    )


def on_device(n_roll, n_fsdp, trainer_weights, power_table, assign):
    own_block = trainer_weights[0]
    centered = (power_table - 125).astype(jnp.bfloat16)
    if n_roll > MOST_SOURCES or n_roll < 4 or n_roll % 2 or n_fsdp & (n_fsdp - 1) or n_fsdp < 2:
        return by_sums(own_block, centered, assign)
    got, table = [], None
    for number in range(assign.shape[0]):
        branches = [
            functools.partial(broadcast, n_roll, n_fsdp, source, number) for source in range(n_roll)
        ]
        if number == 0:
            piece, table = lax.switch(assign[number], branches, own_block, centered)
        else:
            (piece,) = lax.switch(
                assign[number], [functools.partial(lambda g, w: g(w, None), g) for g in branches], own_block
            )
        got.append(piece)
    rollout = jnp.stack(got)
    printed = jnp.einsum("lcd,df->lcf", rollout, table, preferred_element_type=jnp.float32)
    return rollout[None], (printed * spread_inverse).astype(jnp.bfloat16)[None]


def solution(mesh):
    in_specs = (P("roll", None, "fsdp"), P("fsdp", None), P())
    out_specs = (P("roll", None, "fsdp", None), P("roll", None, "fsdp", None))
    return jax.shard_map(
        functools.partial(on_device, mesh.shape["roll"], mesh.shape["fsdp"]),
        mesh=mesh, in_specs=in_specs, out_specs=out_specs, check_vma=False,
    )
```

```python
import functools

import jax
import jax.numpy as jnp
from jax import lax
from jax.experimental import pallas as pl
from jax.experimental.pallas import tpu as pltpu
from jax.sharding import PartitionSpec as P

spread_inverse = 1.0 / 72.0
CHUNKS = 16
MOST_SOURCES = 16
MESH = pl.DeviceIdType.MESH


def flip(index, mask):
    bit = 1
    while bit <= mask:
        if mask & bit:
            index = index + bit - 2 * bit * ((index // bit) % 2)
        bit *= 2
    return index


def powers_below(limit):
    bit, found = 1, []
    while bit < limit:
        found.append(bit)
        bit *= 2
    return found


def broadcast_kernel(n_roll, n_fsdp, source, chunks, with_table, *refs):
    if with_table:
        (w_ref, tab_ref, out_ref, all_ref, stage, local_sem, recv_sem, send_sem, swap_sem, t_local, t_recv, t_send) = refs
    else:
        w_ref, out_ref, stage, local_sem, recv_sem, send_sem, swap_sem = refs
    r, f = lax.axis_index("roll"), lax.axis_index("fsdp")
    half, rungs = n_fsdp // 2, n_roll // 2
    k, b = r // 2, r % 2
    ks, bs = source // 2, source % 2
    pivot = 2 * ks + 1 - bs
    inner = ks + 1 if ks + 1 < rungs else ks - 1
    relay = 2 * inner + 1 - bs
    rows, depth = out_ref.shape[0], w_ref.shape[1]
    height = rows // chunks
    is_source = r == source

    def piece(stream, c, i):
        owner = flip(f, stream * half + i)
        return out_ref.at[
            pl.ds(pl.multiple_of(c * height, height), height),
            pl.ds(pl.multiple_of(owner * depth, 128), depth),
        ]

    def mine(c, owner):
        return w_ref.at[pl.ds(pl.multiple_of(owner * rows + c * height, height), height), :]

    def move(stream, c, i, slot, to, own=False):
        q = c * half + i
        return pltpu.make_async_remote_copy(
            src_ref=mine(c, f) if own else piece(stream, c, i),
            dst_ref=piece(stream, c, i),
            send_sem=send_sem.at[stream, slot, q],
            recv_sem=recv_sem.at[stream, q],
            device_id={"roll": to, "fsdp": f},
            device_id_type=MESH,
        )

    def swap(c, m):
        peer = flip(f, m)
        dst = out_ref.at[
            pl.ds(pl.multiple_of(c * height, height), height),
            pl.ds(pl.multiple_of(f * depth, 128), depth),
        ]
        return pltpu.make_async_remote_copy(
            src_ref=mine(c, peer),
            dst_ref=dst,
            send_sem=swap_sem.at[m - 1, c],
            recv_sem=recv_sem.at[m // half, c * half + m % half],
            device_id={"roll": r, "fsdp": peer},
            device_id_type=MESH,
        )

    def arrived(stream, c, i):
        move(stream, c, i, 0, r).wait_recv()

    def each(body, count=chunks):
        def step(c, carry):
            body(c)
            return carry

        lax.fori_loop(0, count, step, 0)

    up = jnp.logical_and(k >= ks, k + 1 < rungs)
    down = jnp.logical_and(k <= ks, k >= 1)

    t_rows = depth // chunks

    def t_block(c, owner):
        return all_ref.at[pl.ds(pl.multiple_of(owner * depth + c * t_rows, t_rows), t_rows), :]

    def t_move(c, m, slot, to_roll, to_fsdp, m_there):
        owner = flip(f, m)
        src = tab_ref.at[pl.ds(pl.multiple_of(c * t_rows, t_rows), t_rows), :] if m == 0 else t_block(c, owner)
        return pltpu.make_async_remote_copy(
            src_ref=src,
            dst_ref=t_block(c, owner),
            send_sem=t_send.at[m, slot, c],
            recv_sem=t_recv.at[m_there, c],
            device_id={"roll": to_roll, "fsdp": to_fsdp},
            device_id_type=MESH,
        )

    bits = powers_below(n_fsdp)

    def t_own(c, finish):
        for slot, e in enumerate(bits):
            def go(e=e, slot=slot):
                copy = t_move(c, 0, slot, r, flip(f, e), e)
                copy.wait_send() if finish else copy.start()

            if e == half:
                pl.when(jnp.logical_not(is_source))(go)
            else:
                go()

    def t_pass(c, finish):
        for m in range(1, n_fsdp):
            if not finish:
                t_move(c, m, 0, r, f, m).wait_recv()
            for slot, e in enumerate(powers_below(m & -m)):
                copy = t_move(c, m, slot, r, flip(f, e), m + e)
                copy.wait_send() if finish else copy.start()
            if m == half:

                @pl.when(r == pivot)
                def _():
                    copy = t_move(c, m, len(bits), source, f, m)
                    copy.wait_send() if finish else copy.start()

    lag = 2

    def table_step(c):
        if with_table:

            @pl.when(c >= lag)
            def _():
                t_pass(c - lag, False)

    if with_table:
        keep = pltpu.make_async_copy(
            tab_ref, all_ref.at[pl.ds(pl.multiple_of(f * depth, depth), depth), :], t_local
        )
        keep.start()

    @pl.when(is_source)
    def _():
        load = pltpu.make_async_copy(w_ref.at[pl.ds(pl.multiple_of(f * rows, rows), rows), :], stage, local_sem.at[0])
        store = pltpu.make_async_copy(stage, out_ref.at[:, pl.ds(pl.multiple_of(f * depth, 128), depth)], local_sem.at[1])
        load.start()
        ways = ([(0, source + 2)] if ks + 1 < rungs else []) + ([(1, source - 2)] if ks >= 1 else [])

        def begin(c):
            for m in list(range(half, n_fsdp)) + list(range(1, half)):
                swap(c, m).start()
            for slot, to in ways:
                move(0, c, 0, slot, to, own=True).start()
            if with_table:
                t_own(c, False)

        each(begin)

        def step(c):
            for i in range(1, half):
                arrived(0, c, i)
                for slot, to in ways:
                    move(0, c, i, slot, to).start()
            for i in range(half):
                arrived(1, c, i)
                move(1, c, i, 2, pivot).start()
            table_step(c)

        each(step)
        load.wait()
        store.start()
        store.wait()

        def finish(c):
            for m in range(1, n_fsdp):
                swap(c, m).wait_send()
            for slot, to in ways:
                for i in range(half):
                    move(0, c, i, slot, to, own=i == 0).wait_send()
            for i in range(half):
                move(1, c, i, 2, pivot).wait_send()

        each(finish)

    def carry_on(stream, c, i, finish):
        def do(slot, to):
            copy = move(stream, c, i, slot, to)
            copy.wait_send() if finish else copy.start()

        pl.when(up)(lambda: do(0, r + 2))
        pl.when(down)(lambda: do(1, r - 2))
        pl.when(k != ks)(lambda: do(2, r + 1 - 2 * b))

    @pl.when(jnp.logical_not(is_source))
    def _():
        if with_table:
            each(lambda c: t_own(c, False))

    @pl.when(jnp.logical_and(b == bs, k != ks))
    def _():
        def step(c):
            for i in range(half):
                arrived(0, c, i)
                carry_on(0, c, i, False)
            table_step(c)

        each(step)

        def finish(c):
            for i in range(half):
                arrived(1, c, i)
                carry_on(0, c, i, True)

        each(finish)

    @pl.when(b != bs)
    def _():
        def step(c):
            for i in range(half):

                @pl.when(r == relay)
                def _():
                    arrived(0, c, i)
                    move(0, c, i, 0, pivot).start()

                arrived(1, c, i)
                carry_on(1, c, i, False)
            table_step(c)

        each(step)

        def finish(c):
            for i in range(half):

                @pl.when(r == relay)
                def _():
                    move(0, c, i, 0, pivot).wait_send()

                @pl.when(r != relay)
                def _():
                    arrived(0, c, i)

                carry_on(1, c, i, True)

        each(finish)

    if with_table:
        each(lambda c: t_pass(c + chunks - lag, False), lag)

        def finish(c):
            t_own(c, True)
            t_pass(c, True)

        each(finish)
        keep.wait()


def broadcast(n_roll, n_fsdp, source, layer, own_block, table=None):
    rows, depth = own_block.shape[0] // n_fsdp, own_block.shape[1]
    half = n_fsdp // 2
    chunks = min(CHUNKS, rows // 16)
    with_table = table is not None
    anywhere = pl.BlockSpec(memory_space=pl.ANY)
    out_shape = [jax.ShapeDtypeStruct((rows, depth * n_fsdp), own_block.dtype)]
    in_specs = [anywhere]
    scratch = [
        pltpu.VMEM((rows, depth), own_block.dtype),
        pltpu.SemaphoreType.DMA((2,)),
        pltpu.SemaphoreType.DMA((2, chunks * half)),
        pltpu.SemaphoreType.DMA((2, 3, chunks * half)),
        pltpu.SemaphoreType.DMA((n_fsdp - 1, chunks)),
    ]
    operands = [own_block]
    if with_table:
        out_shape.append(jax.ShapeDtypeStruct((depth * n_fsdp, table.shape[1]), table.dtype))
        in_specs.append(pl.BlockSpec(memory_space=pltpu.VMEM))
        scratch += [
            pltpu.SemaphoreType.DMA,
            pltpu.SemaphoreType.DMA((n_fsdp, chunks)),
            pltpu.SemaphoreType.DMA((n_fsdp, len(powers_below(n_fsdp)) + 1, chunks)),
        ]
        operands.append(table)
    return pl.pallas_call(
        functools.partial(broadcast_kernel, n_roll, n_fsdp, source, chunks, with_table),
        out_shape=out_shape,
        in_specs=in_specs,
        out_specs=[anywhere] * len(out_shape),
        scratch_shapes=scratch,
        name=f"broadcast_{layer}_{source}",
        compiler_params=pltpu.CompilerParams(has_side_effects=True),
    )(*operands)


def spread(block, axis, source):
    block = jnp.where(lax.axis_index(axis) == source, block, jnp.zeros_like(block))
    return lax.psum(block, axis)


def by_sums(own_block, centered, assign):
    regrouped = lax.all_to_all(own_block, "fsdp", split_axis=0, concat_axis=1, tiled=True)
    summed = lax.psum_scatter(
        jnp.dot(own_block, centered, preferred_element_type=jnp.float32).astype(jnp.bfloat16),
        "fsdp",
        scatter_dimension=0,
        tiled=True,
    ).astype(jnp.float32)
    printed = (summed * spread_inverse).astype(jnp.bfloat16)
    layers = range(assign.shape[0])
    return (
        jnp.stack([spread(regrouped, "roll", assign[number]) for number in layers])[None],
        jnp.stack([spread(printed, "roll", assign[number]) for number in layers])[None],
    )


def assemble_kernel(n_fsdp, depth, *refs):
    *got_refs, rollout_ref, printed_ref, total = refs
    step = pl.program_id(1)
    for layer, got_ref in enumerate(got_refs):
        rollout_ref[layer] = got_ref[:, :depth]
        term = got_ref[:, depth:].astype(jnp.float32)

        @pl.when(step == 0)
        def _():
            total[layer] = term

        @pl.when(step > 0)
        def _():
            total[layer] += term

        @pl.when(step == n_fsdp - 1)
        def _():
            printed_ref[layer] = (total[layer] * spread_inverse).astype(jnp.bfloat16)


def assemble(got, n_fsdp, depth, width):
    layers, rows = len(got), got[0].shape[0]
    tile = rows // 2
    return pl.pallas_call(
        functools.partial(assemble_kernel, n_fsdp, depth),
        grid=(rows // tile, n_fsdp),
        in_specs=[pl.BlockSpec((tile, depth + width), lambda i, j: (i, j))] * layers,
        out_specs=[
            pl.BlockSpec((layers, tile, depth), lambda i, j: (0, i, j)),
            pl.BlockSpec((layers, tile, width), lambda i, j: (0, i, 0)),
        ],
        out_shape=[
            jax.ShapeDtypeStruct((layers, rows, depth * n_fsdp), jnp.bfloat16),
            jax.ShapeDtypeStruct((layers, rows, width), jnp.bfloat16),
        ],
        scratch_shapes=[pltpu.VMEM((layers, tile, width), jnp.float32)],
        name="assemble",
    )(*got)


def on_device(n_roll, n_fsdp, trainer_weights, power_table, assign):
    own_block = trainer_weights[0]
    centered = (power_table - 125).astype(jnp.bfloat16)
    if n_roll > MOST_SOURCES or n_roll < 4 or n_roll % 2 or n_fsdp & (n_fsdp - 1) or n_fsdp < 2:
        return by_sums(own_block, centered, assign)
    depth, width = own_block.shape[1], centered.shape[1]
    partial = jnp.dot(own_block, centered, preferred_element_type=jnp.float32).astype(jnp.bfloat16)
    joined = jnp.concatenate([own_block, partial], axis=1)
    got = []
    for number in range(assign.shape[0]):
        branches = [
            functools.partial(broadcast, n_roll, n_fsdp, source, number) for source in range(n_roll)
        ]
        got.append(lax.switch(assign[number], branches, joined)[0])
    rollout, printed = assemble(got, n_fsdp, depth, width)
    return rollout[None], printed[None]


def solution(mesh):
    in_specs = (P("roll", None, "fsdp"), P("fsdp", None), P())
    out_specs = (P("roll", None, "fsdp", None), P("roll", None, "fsdp", None))
    return jax.shard_map(
        functools.partial(on_device, mesh.shape["roll"], mesh.shape["fsdp"]),
        mesh=mesh, in_specs=in_specs, out_specs=out_specs, check_vma=False,
    )
```

```python
import functools

import jax
import jax.numpy as jnp
from jax import lax
from jax.experimental import pallas as pl
from jax.experimental.pallas import tpu as pltpu
from jax.sharding import PartitionSpec as P

spread_inverse = 1.0 / 72.0
CHUNKS = 16
MOST_SOURCES = 16
MESH = pl.DeviceIdType.MESH


def flip(index, mask):
    bit = 1
    while bit <= mask:
        if mask & bit:
            index = index + bit - 2 * bit * ((index // bit) % 2)
        bit *= 2
    return index


def powers_below(limit):
    bit, found = 1, []
    while bit < limit:
        found.append(bit)
        bit *= 2
    return found


def broadcast_kernel(n_roll, n_fsdp, source, chunks, with_table, *refs):
    if with_table:
        (w_ref, tab_ref, out_ref, all_ref, stage, local_sem, recv_sem, send_sem, swap_sem, t_local, t_recv, t_send) = refs
    else:
        w_ref, out_ref, stage, local_sem, recv_sem, send_sem, swap_sem = refs
    r, f = lax.axis_index("roll"), lax.axis_index("fsdp")
    half, rungs = n_fsdp // 2, n_roll // 2
    k, b = r // 2, r % 2
    ks, bs = source // 2, source % 2
    pivot = 2 * ks + 1 - bs
    inner = ks + 1 if ks + 1 < rungs else ks - 1
    relay = 2 * inner + 1 - bs
    rows, depth = out_ref.shape[0], w_ref.shape[1]
    height = rows // chunks
    is_source = r == source

    def piece(stream, c, i):
        owner = flip(f, stream * half + i)
        return out_ref.at[
            pl.ds(pl.multiple_of(c * height, height), height),
            pl.ds(pl.multiple_of(owner * depth, 128), depth),
        ]

    def mine(c, owner):
        return w_ref.at[pl.ds(pl.multiple_of(owner * rows + c * height, height), height), :]

    def move(stream, c, i, slot, to, own=False):
        q = c * half + i
        return pltpu.make_async_remote_copy(
            src_ref=mine(c, f) if own else piece(stream, c, i),
            dst_ref=piece(stream, c, i),
            send_sem=send_sem.at[stream, slot, q],
            recv_sem=recv_sem.at[stream, q],
            device_id={"roll": to, "fsdp": f},
            device_id_type=MESH,
        )

    def swap(c, m):
        peer = flip(f, m)
        dst = out_ref.at[
            pl.ds(pl.multiple_of(c * height, height), height),
            pl.ds(pl.multiple_of(f * depth, 128), depth),
        ]
        return pltpu.make_async_remote_copy(
            src_ref=mine(c, peer),
            dst_ref=dst,
            send_sem=swap_sem.at[m - 1, c],
            recv_sem=recv_sem.at[m // half, c * half + m % half],
            device_id={"roll": r, "fsdp": peer},
            device_id_type=MESH,
        )

    def arrived(stream, c, i):
        move(stream, c, i, 0, r).wait_recv()

    def each(body, count=chunks):
        def step(c, carry):
            body(c)
            return carry

        lax.fori_loop(0, count, step, 0)

    up = jnp.logical_and(k >= ks, k + 1 < rungs)
    down = jnp.logical_and(k <= ks, k >= 1)

    t_rows = depth // chunks

    def t_block(c, owner):
        return all_ref.at[pl.ds(pl.multiple_of(owner * depth + c * t_rows, t_rows), t_rows), :]

    def t_move(c, m, slot, to_roll, to_fsdp, m_there):
        owner = flip(f, m)
        src = tab_ref.at[pl.ds(pl.multiple_of(c * t_rows, t_rows), t_rows), :] if m == 0 else t_block(c, owner)
        return pltpu.make_async_remote_copy(
            src_ref=src,
            dst_ref=t_block(c, owner),
            send_sem=t_send.at[m, slot, c],
            recv_sem=t_recv.at[m_there, c],
            device_id={"roll": to_roll, "fsdp": to_fsdp},
            device_id_type=MESH,
        )

    bits = powers_below(n_fsdp)

    def t_own(c, finish):
        for slot, e in enumerate(bits):
            def go(e=e, slot=slot):
                copy = t_move(c, 0, slot, r, flip(f, e), e)
                copy.wait_send() if finish else copy.start()

            if e == half:
                pl.when(jnp.logical_not(is_source))(go)
            else:
                go()

    def t_pass(c, finish):
        for m in range(1, n_fsdp):
            if not finish:
                t_move(c, m, 0, r, f, m).wait_recv()
            for slot, e in enumerate(powers_below(m & -m)):
                copy = t_move(c, m, slot, r, flip(f, e), m + e)
                copy.wait_send() if finish else copy.start()
            if m == half:

                @pl.when(r == pivot)
                def _():
                    copy = t_move(c, m, len(bits), source, f, m)
                    copy.wait_send() if finish else copy.start()

    lag = 2

    def table_step(c):
        if with_table:

            @pl.when(c >= lag)
            def _():
                t_pass(c - lag, False)

    if with_table:
        keep = pltpu.make_async_copy(
            tab_ref, all_ref.at[pl.ds(pl.multiple_of(f * depth, depth), depth), :], t_local
        )
        keep.start()

    @pl.when(is_source)
    def _():
        load = pltpu.make_async_copy(w_ref.at[pl.ds(pl.multiple_of(f * rows, rows), rows), :], stage, local_sem.at[0])
        store = pltpu.make_async_copy(stage, out_ref.at[:, pl.ds(pl.multiple_of(f * depth, 128), depth)], local_sem.at[1])
        load.start()
        ways = ([(0, source + 2)] if ks + 1 < rungs else []) + ([(1, source - 2)] if ks >= 1 else [])

        def begin(c):
            for m in list(range(half, n_fsdp)) + list(range(1, half)):
                swap(c, m).start()
            for slot, to in ways:
                move(0, c, 0, slot, to, own=True).start()
            if with_table:
                t_own(c, False)

        lead = min(3, chunks)
        each(begin, lead)

        def step(c):
            pl.when(c + lead < chunks)(lambda: begin(c + lead))
            for i in range(1, half):
                arrived(0, c, i)
                for slot, to in ways:
                    move(0, c, i, slot, to).start()
            for i in range(half):
                arrived(1, c, i)
                move(1, c, i, 2, pivot).start()
            table_step(c)

        each(step)
        load.wait()
        store.start()
        store.wait()

        def finish(c):
            for m in range(1, n_fsdp):
                swap(c, m).wait_send()
            for slot, to in ways:
                for i in range(half):
                    move(0, c, i, slot, to, own=i == 0).wait_send()
            for i in range(half):
                move(1, c, i, 2, pivot).wait_send()

        each(finish)

    def carry_on(stream, c, i, finish):
        def do(slot, to):
            copy = move(stream, c, i, slot, to)
            copy.wait_send() if finish else copy.start()

        pl.when(up)(lambda: do(0, r + 2))
        pl.when(down)(lambda: do(1, r - 2))
        pl.when(k != ks)(lambda: do(2, r + 1 - 2 * b))

    @pl.when(jnp.logical_not(is_source))
    def _():
        if with_table:
            each(lambda c: t_own(c, False))

    @pl.when(jnp.logical_and(b == bs, k != ks))
    def _():
        def step(c):
            for i in range(half):
                arrived(0, c, i)
                carry_on(0, c, i, False)
            table_step(c)

        each(step)

        def finish(c):
            for i in range(half):
                arrived(1, c, i)
                carry_on(0, c, i, True)

        each(finish)

    @pl.when(b != bs)
    def _():
        def step(c):
            for i in range(half):

                @pl.when(r == relay)
                def _():
                    arrived(0, c, i)
                    move(0, c, i, 0, pivot).start()

                arrived(1, c, i)
                carry_on(1, c, i, False)
            table_step(c)

        each(step)

        def finish(c):
            for i in range(half):

                @pl.when(r == relay)
                def _():
                    move(0, c, i, 0, pivot).wait_send()

                @pl.when(r != relay)
                def _():
                    arrived(0, c, i)

                carry_on(1, c, i, True)

        each(finish)

    if with_table:
        each(lambda c: t_pass(c + chunks - lag, False), lag)

        def finish(c):
            t_own(c, True)
            t_pass(c, True)

        each(finish)
        keep.wait()


def broadcast(n_roll, n_fsdp, source, layer, own_block, table=None):
    rows, depth = own_block.shape[0] // n_fsdp, own_block.shape[1]
    half = n_fsdp // 2
    chunks = min(CHUNKS, rows // 16)
    with_table = table is not None
    anywhere = pl.BlockSpec(memory_space=pl.ANY)
    out_shape = [jax.ShapeDtypeStruct((rows, depth * n_fsdp), own_block.dtype)]
    in_specs = [anywhere]
    scratch = [
        pltpu.VMEM((rows, depth), own_block.dtype),
        pltpu.SemaphoreType.DMA((2,)),
        pltpu.SemaphoreType.DMA((2, chunks * half)),
        pltpu.SemaphoreType.DMA((2, 3, chunks * half)),
        pltpu.SemaphoreType.DMA((n_fsdp - 1, chunks)),
    ]
    operands = [own_block]
    if with_table:
        out_shape.append(jax.ShapeDtypeStruct((depth * n_fsdp, table.shape[1]), table.dtype))
        in_specs.append(pl.BlockSpec(memory_space=pltpu.VMEM))
        scratch += [
            pltpu.SemaphoreType.DMA,
            pltpu.SemaphoreType.DMA((n_fsdp, chunks)),
            pltpu.SemaphoreType.DMA((n_fsdp, len(powers_below(n_fsdp)) + 1, chunks)),
        ]
        operands.append(table)
    return pl.pallas_call(
        functools.partial(broadcast_kernel, n_roll, n_fsdp, source, chunks, with_table),
        out_shape=out_shape,
        in_specs=in_specs,
        out_specs=[anywhere] * len(out_shape),
        scratch_shapes=scratch,
        name=f"broadcast_{layer}_{source}",
        compiler_params=pltpu.CompilerParams(has_side_effects=True),
    )(*operands)


def spread(block, axis, source):
    block = jnp.where(lax.axis_index(axis) == source, block, jnp.zeros_like(block))
    return lax.psum(block, axis)


def by_sums(own_block, centered, assign):
    regrouped = lax.all_to_all(own_block, "fsdp", split_axis=0, concat_axis=1, tiled=True)
    summed = lax.psum_scatter(
        jnp.dot(own_block, centered, preferred_element_type=jnp.float32).astype(jnp.bfloat16),
        "fsdp",
        scatter_dimension=0,
        tiled=True,
    ).astype(jnp.float32)
    printed = (summed * spread_inverse).astype(jnp.bfloat16)
    layers = range(assign.shape[0])
    return (
        jnp.stack([spread(regrouped, "roll", assign[number]) for number in layers])[None],
        jnp.stack([spread(printed, "roll", assign[number]) for number in layers])[None],
    )


def assemble_kernel(n_fsdp, depth, *refs):
    *got_refs, rollout_ref, printed_ref, total = refs
    step = pl.program_id(1)
    for layer, got_ref in enumerate(got_refs):
        rollout_ref[layer] = got_ref[:, :depth]
        term = got_ref[:, depth:].astype(jnp.float32)

        @pl.when(step == 0)
        def _():
            total[layer] = term

        @pl.when(step > 0)
        def _():
            total[layer] += term

        @pl.when(step == n_fsdp - 1)
        def _():
            printed_ref[layer] = (total[layer] * spread_inverse).astype(jnp.bfloat16)


def assemble(got, n_fsdp, depth, width):
    layers, rows = len(got), got[0].shape[0]
    tile = rows // 2
    return pl.pallas_call(
        functools.partial(assemble_kernel, n_fsdp, depth),
        grid=(rows // tile, n_fsdp),
        in_specs=[pl.BlockSpec((tile, depth + width), lambda i, j: (i, j))] * layers,
        out_specs=[
            pl.BlockSpec((layers, tile, depth), lambda i, j: (0, i, j)),
            pl.BlockSpec((layers, tile, width), lambda i, j: (0, i, 0)),
        ],
        out_shape=[
            jax.ShapeDtypeStruct((layers, rows, depth * n_fsdp), jnp.bfloat16),
            jax.ShapeDtypeStruct((layers, rows, width), jnp.bfloat16),
        ],
        scratch_shapes=[pltpu.VMEM((layers, tile, width), jnp.float32)],
        name="assemble",
    )(*got)


def on_device(n_roll, n_fsdp, trainer_weights, power_table, assign):
    own_block = trainer_weights[0]
    centered = (power_table - 125).astype(jnp.bfloat16)
    if n_roll > MOST_SOURCES or n_roll < 4 or n_roll % 2 or n_fsdp & (n_fsdp - 1) or n_fsdp < 2:
        return by_sums(own_block, centered, assign)
    depth, width = own_block.shape[1], centered.shape[1]
    partial = jnp.dot(own_block, centered, preferred_element_type=jnp.float32).astype(jnp.bfloat16)
    joined = jnp.concatenate([own_block, partial], axis=1)
    got = []
    for number in range(assign.shape[0]):
        branches = [
            functools.partial(broadcast, n_roll, n_fsdp, source, number) for source in range(n_roll)
        ]
        got.append(lax.switch(assign[number], branches, joined)[0])
    rollout, printed = assemble(got, n_fsdp, depth, width)
    return rollout[None], printed[None]


def solution(mesh):
    in_specs = (P("roll", None, "fsdp"), P("fsdp", None), P())
    out_specs = (P("roll", None, "fsdp", None), P("roll", None, "fsdp", None))
    return jax.shard_map(
        functools.partial(on_device, mesh.shape["roll"], mesh.shape["fsdp"]),
        mesh=mesh, in_specs=in_specs, out_specs=out_specs, check_vma=False,
    )
```
